32 devices in a mesh: sub: 2 (over core), brick: 16 (over z, y, x).
Axes of the slice: x: 2, y: 2, z: 4, core: 2. Of those that a mesh axis runs over, the one named last changes fastest.
Arguments:
- increments: float32 [4, 128, 256, 512], P('sub', None, 'brick'), may hold values from -6 to 6
- courant_x: float32 [4, 128, 256, 512], P('sub', None, 'brick'), may hold values from -0.5 to 0.5
- courant_y: float32 [4, 128, 256, 512], P('sub', None, 'brick'), may hold values from -0.5 to 0.5
- spectrum: float32 [256, 512], replicated, may hold values from 0.05 to 2
- vertical: float32 [128, 128], replicated, may hold values from -0.5 to 0.5
Outputs:
- covaried: float32 [4, 128, 256, 512], P('sub', None, 'brick')
The draws below stay inside these ranges and needn't reach their ends.
All inputs are finite; a program needn't handle non-finite values.
Results may differ from the reference program's by a relative error of at most 0.00007.
Values sent between devices are 32-bit elements; how exact they have to be, the bound alone decides.
No kernel may reach another device: no remote copies, remote signals or barrier semaphores. Data moves between devices by JAX's collectives and lax.ppermute only.
A program may use at most 192 MiB of HBM per device.

```python
import math
import jax
import jax.numpy as jnp
from jax import lax

NX = 256
NY = 512
L = 128
STEPS = 4
SUBS = 4


def levels(own_key, dims, shards, least, largest):
    level = 1.0
    for position, parts in shards:
        heights = jax.random.uniform(jax.random.fold_in(jax.random.fold_in(own_key, 6), position), (parts,), jnp.float32, least / len(shards), largest / len(shards))
        level = level * jnp.repeat(jnp.exp(heights), dims[position] // parts).reshape((-1,) + (1,) * (len(dims) - 1 - position))
    return level


def noise(rng, dims, spread, bound, pieces=(), kind=jnp.bfloat16):
    array = jax.random.normal(rng, dims, jnp.float32) * spread
    if len(pieces) > 0:
        array = levels(rng, dims, pieces, -0.22, 0.18) * array
    return jnp.clip(array, min=-bound, max=bound).astype(kind)


def setup_inputs(seed: int = 0) -> dict:
    streams_of = jax.random.split(jax.random.key(seed), 6)
    increments = noise(streams_of[0], (SUBS, L, NX, NY), 1.0, 6.0, ((0, 2), (2, 16)), jnp.float32)
    courant_x = jnp.clip(jax.random.uniform(streams_of[1], (SUBS, L, NX, NY), jnp.float32, -0.5, 0.5) * levels(streams_of[1], (SUBS, L, NX, NY), ((0, 2), (2, 16)), -0.4, 0.0), -0.5, 0.5)
    courant_y = jnp.clip(jax.random.uniform(streams_of[2], (SUBS, L, NX, NY), jnp.float32, -0.5, 0.5) * levels(streams_of[2], (SUBS, L, NX, NY), ((0, 2), (2, 16)), -0.4, 0.0), -0.5, 0.5)
    spectrum = jnp.clip(jnp.exp(jax.random.uniform(streams_of[3], (NX, NY), jnp.float32, math.log(0.05), math.log(2.0))), 0.05, 2.0)
    vertical = noise(streams_of[4], (L, L), L ** -0.5, 0.5, (), jnp.float32)
    return dict(increments=increments, courant_x=courant_x, courant_y=courant_y, spectrum=spectrum, vertical=vertical)


diffusion = 0.2

def dct_table(count):
    freq = jnp.arange(count, dtype=jnp.float32)[:, None]
    cells = jnp.arange(count, dtype=jnp.float32)[None, :]
    table = jnp.cos(jnp.pi * (cells + 0.5) * freq / count) * jnp.sqrt(jnp.float32(2.0) / count)
    first = jnp.where(jnp.arange(count)[:, None] == 0, jnp.sqrt(jnp.float32(0.5)), jnp.float32(1.0))
    return table * first

def advance(extended, courant_x, courant_y):
    center = extended[..., 1:-1, :]
    north = extended[..., 2:, :]
    south = extended[..., :-2, :]
    widths = [(0, 0)] * (center.ndim - 1) + [(1, 1)]
    padded = jnp.pad(center, widths)
    east = padded[..., 2:]
    west = padded[..., :-2]
    return center - 0.5 * courant_x * (north - south) - 0.5 * courant_y * (east - west) + diffusion * (north + south + east + west - 4.0 * center)

def propagate(triple):
    state, speed_x, speed_y = triple
    for number in range(STEPS):
        extended = jnp.pad(state, ((0, 0), (1, 1), (0, 0)))
        state = advance(extended, speed_x, speed_y)
    return state

def reference(increments, courant_x, courant_y, spectrum, vertical):
    ends = lax.map(propagate, (increments, courant_x, courant_y))
    previous = jnp.concatenate([jnp.zeros_like(ends[:1]), ends[:-1]], axis=0)
    jumps = increments - previous
    row_table = dct_table(NX)
    col_table = dct_table(NY)
    high = lax.Precision.HIGHEST

    def covary(block):
        forward = jnp.einsum('kx,lxy->lky', row_table, block, precision=high)
        forward = jnp.einsum('lky,jy->lkj', forward, col_table, precision=high)
        scaled = forward * spectrum
        back = jnp.einsum('lkj,jy->lky', scaled, col_table, precision=high)
        back = jnp.einsum('kx,lky->lxy', row_table, back, precision=high)
        return jnp.einsum('ml,lxy->mxy', vertical, back, precision=high)
    return lax.map(covary, jumps)
```

```python
import functools

import jax
import jax.numpy as jnp
from jax import lax
from jax.experimental import pallas as pl
from jax.experimental.pallas import tpu as pltpu
from jax.sharding import PartitionSpec as P

STEPS = 4
LANES = 128
DIFFUSION = 0.2
CUTS_LAST = (4, 8)
CUTS_FIRST = (8,)


def dct_table(count):
    freq = jnp.arange(count, dtype=jnp.float32)[:, None]
    cells = jnp.arange(count, dtype=jnp.float32)[None, :]
    table = jnp.cos(jnp.pi * (cells + 0.5) * freq / count) * jnp.sqrt(jnp.float32(2.0) / count)
    first = jnp.where(jnp.arange(count)[:, None] == 0, jnp.sqrt(jnp.float32(0.5)), jnp.float32(1.0))
    return table * first


def halves(table):
    high = lax.reduce_precision(table, 8, 7)
    return high.astype(jnp.bfloat16), (table - high).astype(jnp.bfloat16)


def split(value):
    high = value.astype(jnp.bfloat16)
    return high, (value - high.astype(jnp.float32)).astype(jnp.bfloat16)


def dot3(left, right):
    dot = functools.partial(jnp.dot, preferred_element_type=jnp.float32)
    return dot(left[0], right[0]) + (dot(left[0], right[1]) + dot(left[1], right[0]))


def stepped(center, north, south, half_x, half_y):
    cols = center.shape[1]
    lane = lax.broadcasted_iota(jnp.int32, center.shape, 1)
    east = jnp.where(lane == cols - 1, 0.0, pltpu.roll(center, cols - 1, 1))
    west = jnp.where(lane == 0, 0.0, pltpu.roll(center, 1, 1))
    total = (north + south) + (east + west) + center
    return DIFFUSION * total - half_x * (north - south) - half_y * (east - west)


def tangent_kernel(rows, parts, first, last, *refs):
    refs = list(refs)

    def take(count):
        taken = refs[:count]
        del refs[:count]
        return taken

    (inside,) = take(1)
    state = take(parts) if first else take(1)[0]
    cx, cy = take(parts), take(parts)
    before, after = take(2)
    far_before, far_after = (before, after) if first else take(2)
    target = take(parts) if last == "jump" else None
    (out,) = take(1)
    old, mid, hx, hy, flat = refs
    at = lambda i: slice(i * LANES, (i + 1) * LANES)

    def gather(pieces, x):
        return jnp.concatenate([p[pl.ds(x, 8, stride=rows), :] for p in pieces], axis=1)

    for x in range(rows):
        old[x + 2] = gather(state, x) if first else state[x]
        hx[x + 1] = 0.5 * gather(cx, x)
        hy[x + 1] = 0.5 * gather(cy, x)
    for h in range(2):
        old[h] = before[h]
        old[rows + 2 + h] = after[h]
    hx[0], hy[0] = 0.5 * far_before[2], 0.5 * far_before[3]
    hx[rows + 1], hy[rows + 1] = 0.5 * far_after[2], 0.5 * far_after[3]
    for x in range(rows + 2):
        new = stepped(old[x + 1], old[x + 2], old[x], hx[x], hy[x])
        if x == 0:
            new = new * inside[0]
        if x == rows + 1:
            new = new * inside[1]
        mid[x] = new
    for x in range(rows):
        new = stepped(mid[x + 1], mid[x + 2], mid[x], hx[x + 1], hy[x + 1])
        if not last:
            out[x] = new
        else:
            for i in range(parts):
                flat[i, pl.ds(x, 8, stride=rows), :] = new[:, at(i)]
    if last:
        for i in range(parts):
            out[:, at(i)] = target[i][...] - flat[i] if target else flat[i]


def mid_kernel(block_ref, spectrum_ref, rh, rl, rth, rtl, ch, cl, cth, ctl, out_ref):
    count, _, rows, cols = block_ref.shape
    field = block_ref[...].reshape(count * rows, cols)
    along_y = dot3(split(field), (cth[...], ctl[...]))
    full = dot3((rh[...], rl[...]), split(along_y)) * spectrum_ref[...]
    back = dot3((rth[...], rtl[...]), split(full))
    out_ref[...] = dot3(split(back), (ch[...], cl[...])).reshape(count, 1, rows, cols)


def mix_kernel(rows, field_ref, vh_ref, vl_ref, *refs):
    out_ref = refs[-1]
    levels = vh_ref.shape[1]
    factor = (vh_ref[...], vl_ref[...])
    for x in range(rows):
        field = field_ref[pl.ds(x, levels, stride=rows), :]
        out_ref[pl.ds(x, levels, stride=rows), :] = dot3(factor, split(field))


def params(**more):
    return pltpu.CompilerParams(vmem_limit_bytes=56 << 20, **more)


def on_device(increments, courant_x, courant_y, spectrum, vertical):
    subs, levels, rows, cols = increments.shape
    bricks, groups = lax.axis_size("brick"), lax.axis_size("sub")
    brick = lax.axis_index("brick")
    f32 = jnp.float32

    def neighbour(value, by, part_of_end):
        pairs = []
        for g in range(groups - 1 if part_of_end else groups):
            pairs += [(g * bricks + i, g * bricks + i + by) for i in range(bricks) if 0 <= i + by < bricks]
        return lax.ppermute(value, ("sub", "brick"), pairs)

    def next_sub(value):
        return lax.ppermute(value, "sub", [(i, i + 1) for i in range(groups - 1)])

    row_table, col_table = dct_table(rows * bricks), dct_table(cols)
    tables = (*halves(row_table), *halves(row_table.T), *halves(col_table), *halves(col_table.T))

    def cost(values, passes):
        return pl.CostEstimate(flops=20 * values * passes, bytes_accessed=16 * values * passes, transcendentals=0)

    def chunk_of(cuts):
        ends = [max(1, round(c * (levels // bricks) / 8)) * bricks for c in cuts]
        return [(a, b) for a, b in zip([0] + ends[:-1], ends) if b > a]

    parts = cols // LANES
    flat_all = [a.reshape(-1, cols) for a in (increments, courant_x, courant_y)]
    inside = jnp.stack([jnp.where(brick > 0, 1.0, 0.0), jnp.where(brick < bricks - 1, 1.0, 0.0)]).astype(f32)

    def pieces(array, sub, start):
        specs = [
            pl.BlockSpec((8 * rows, LANES), lambda i, j=j: ((sub * levels + start) // 8 + i, j)) for j in range(parts)
        ]
        return [array] * parts, specs

    def first_halo(sub, start, stop):
        inc, cx, cy = (a[sub, start:stop] for a in (increments, courant_x, courant_y))
        last = sub == subs - 1
        low = jnp.stack([inc[:, rows - 2], inc[:, rows - 1], cx[:, rows - 1], cy[:, rows - 1]])
        high = jnp.stack([inc[:, 0], inc[:, 1], cx[:, 0], cy[:, 0]])
        return neighbour(low, 1, last), neighbour(high, -1, last)

    def tangent(number, sub, start, stop, state, halo, far, target):
        span = stop - start
        first = number == 0
        last = None if first else ("end" if target is None else "jump")
        slab = pl.BlockSpec((rows, 8, cols), lambda i: (0, i, 0))
        inputs, specs = [inside], [pl.BlockSpec(memory_space=pltpu.SMEM)]

        def add(more, with_specs):
            inputs.extend(more)
            specs.extend(with_specs)

        if first:
            add(*pieces(flat_all[0], sub, start))
        else:
            add([state], [slab])
        add(*pieces(flat_all[1], sub, start))
        add(*pieces(flat_all[2], sub, start))
        for pair in (halo,) if first else (halo, far):
            add(pair, [pl.BlockSpec((pair[0].shape[0], 8, cols), lambda i: (0, i, 0))] * 2)
        if last == "jump":
            add(*pieces(flat_all[0], target, start))
        if first:
            out, out_spec = (rows, span, cols), slab
        else:
            out, out_spec = (span * rows, cols), pl.BlockSpec((8 * rows, cols), lambda i: (i, 0))
        return pl.pallas_call(
            functools.partial(tangent_kernel, rows, parts, first, last),
            grid=(span // 8,),
            in_specs=specs,
            out_specs=out_spec,
            out_shape=jax.ShapeDtypeStruct(out, f32),
            scratch_shapes=[
                pltpu.VMEM((rows + 4, 8, cols), f32),
                pltpu.VMEM((rows + 2, 8, cols), f32),
                pltpu.VMEM((rows + 2, 8, cols), f32),
                pltpu.VMEM((rows + 2, 8, cols), f32),
                pltpu.VMEM((parts, 8 * rows, LANES), f32),
            ],
            compiler_params=params(),
            cost_estimate=cost(span * rows * cols, 2),
            name="tangent",
        )(*inputs)

    def advance(sub, target, start, stop):
        far = first_halo(sub, start, stop)
        state = tangent(0, sub, start, stop, None, far, far, None)
        last = sub == subs - 1
        halo = neighbour(state[rows - 2 :], 1, last), neighbour(state[:2], -1, last)
        return tangent(1, sub, start, stop, state, halo, far, target).reshape(stop - start, rows, cols)

    def spread(value):
        return lax.all_to_all(value, "brick", split_axis=0, concat_axis=0, tiled=True)

    def middle(block, done, offset, total):
        share = block.shape[0] // bricks
        block = block.reshape(bricks, share, rows, cols)
        fixed = [pl.BlockSpec(t.shape, lambda i: (0, 0), pipeline_mode=pl.Buffered(1)) for t in (spectrum, *tables)]
        piece = pl.BlockSpec((bricks, 1, rows, cols), lambda i: (0, i, 0, 0))
        flops = 12 * share * bricks * rows * cols * (cols + bricks * rows)
        inputs = [block, spectrum, *tables]
        specs = [piece] + fixed
        kernel, alias = mid_kernel, {}
        if done is not None:
            alias = {len(inputs): 0}
            inputs.append(done)
            specs.append(pl.BlockSpec(memory_space=pl.ANY))
            kernel = lambda *refs: mid_kernel(*refs[:-2], refs[-1])
        return pl.pallas_call(
            kernel,
            grid=(share,),
            in_specs=specs,
            out_specs=pl.BlockSpec((bricks, 1, rows, cols), lambda i: (0, i + offset, 0, 0)),
            out_shape=jax.ShapeDtypeStruct((bricks, total, rows, cols), f32),
            input_output_aliases=alias,
            compiler_params=params(),
            cost_estimate=pl.CostEstimate(flops=flops, bytes_accessed=8 * block.size, transcendentals=0),
            name="middle",
        )(*inputs)

    def mix(field, sub, factor, old):
        field = field.reshape(levels * rows, cols)
        inputs = [field, *factor]
        whole = pl.BlockSpec((levels, levels), lambda i: (0, 0))
        specs = [pl.BlockSpec((levels * rows, LANES), lambda i: (0, i)), whole, whole]
        kernel, alias = functools.partial(mix_kernel, rows), {}
        if old is not None:
            inputs.append(old)
            specs.append(pl.BlockSpec(memory_space=pl.ANY))
            alias = {3: 0}
        return pl.pallas_call(
            kernel,
            grid=(parts,),
            in_specs=specs,
            out_specs=pl.BlockSpec((levels * rows, LANES), lambda i: (sub, i)),
            out_shape=jax.ShapeDtypeStruct((subs * levels * rows, cols), f32),
            input_output_aliases=alias,
            compiler_params=params(),
            cost_estimate=pl.CostEstimate(
                flops=6 * levels * levels * rows * cols, bytes_accessed=8 * levels * rows * cols, transcendentals=0
            ),
            name="mix",
        )(*inputs)

    out = None
    work = []
    for target in range(subs - 1, 0, -1):
        cuts = chunk_of(CUTS_LAST if target == subs - 1 else CUTS_FIRST)
        work.append((target, [(a, b, advance(target - 1, target, a, b)) for a, b in cuts]))
    ends = [(a, b, advance(subs - 1, None, a, b)) for a, b in chunk_of(CUTS_FIRST)]
    work.append((0, [(a, b, increments[0, a:b] - next_sub(e)) for a, b, e in ends]))
    received = [(sub, [(a, b, spread(jump)) for a, b, jump in group]) for sub, group in work]
    returned = []
    for sub, group in received:
        done, offset, columns = None, 0, []
        for a, b, block in group:
            share = (b - a) // bricks
            done = middle(block, done, offset, levels // bricks)
            offset += share
            columns.append(vertical[:, a:b].reshape(levels, bricks, share))
        factor = jnp.concatenate(columns, axis=2).reshape(levels, levels)
        returned.append((sub, halves(factor), spread(done)))
    for sub, factor, part in returned:
        out = mix(part, sub, factor, out)
    return out.reshape(increments.shape)


def solution(mesh):
    spec = P("sub", None, "brick", None)
    return jax.shard_map(
        on_device, mesh=mesh, in_specs=(spec, spec, spec, P(), P()), out_specs=spec, check_vma=False
    )
```

```python
import functools

import jax
import jax.numpy as jnp
from jax import lax
from jax.experimental import pallas as pl
from jax.experimental.pallas import tpu as pltpu
from jax.sharding import PartitionSpec as P


LANES = 128
DIFFUSION = 0.2
CUTS_LAST = (4, 8)
CUTS_FIRST = (8,)


def dct_table(count):
    freq = jnp.arange(count, dtype=jnp.float32)[:, None]
    cells = jnp.arange(count, dtype=jnp.float32)[None, :]
    table = jnp.cos(jnp.pi * (cells + 0.5) * freq / count) * jnp.sqrt(jnp.float32(2.0) / count)
    first = jnp.where(jnp.arange(count)[:, None] == 0, jnp.sqrt(jnp.float32(0.5)), jnp.float32(1.0))
    return table * first


def halves(table):
    high = lax.reduce_precision(table, 8, 7)
    return high.astype(jnp.bfloat16), (table - high).astype(jnp.bfloat16)


def split(value):
    high = value.astype(jnp.bfloat16)
    return high, (value - high.astype(jnp.float32)).astype(jnp.bfloat16)


def dot3(left, right):
    dot = functools.partial(jnp.dot, preferred_element_type=jnp.float32)
    return dot(left[0], right[0]) + (dot(left[0], right[1]) + dot(left[1], right[0]))


def stepped(center, north, south, half_x, half_y):
    cols = center.shape[1]
    lane = lax.broadcasted_iota(jnp.int32, center.shape, 1)
    east = jnp.where(lane == cols - 1, 0.0, pltpu.roll(center, cols - 1, 1))
    west = jnp.where(lane == 0, 0.0, pltpu.roll(center, 1, 1))
    total = (north + south) + (east + west) + center
    return DIFFUSION * total - half_x * (north - south) - half_y * (east - west)


def edge_kernel(inc_b, cx_b, cy_b, inc_t, cx_t, cy_t, low, high):
    low[0], low[1] = inc_b[:, 6, :], inc_b[:, 7, :]
    low[2], low[3] = cx_b[:, 7, :], cy_b[:, 7, :]
    high[0], high[1] = inc_t[:, 0, :], inc_t[:, 1, :]
    high[2], high[3] = cx_t[:, 0, :], cy_t[:, 0, :]


def tangent_kernel(rows, parts, first, last, *refs):
    refs = list(refs)

    def take(count):
        taken = refs[:count]
        del refs[:count]
        return taken

    (inside,) = take(1)
    state = take(parts) if first else take(1)[0]
    cx, cy = take(parts), take(parts)
    before, after = take(2)
    far_before, far_after = (before, after) if first else take(2)
    target = take(parts) if last == "jump" else None
    (out,) = take(1)
    low, high = (None, None) if last else take(2)
    old, mid, hx, hy, flat = refs
    at = lambda i: slice(i * LANES, (i + 1) * LANES)

    def gather(pieces, x):
        return jnp.concatenate([p[pl.ds(x, 8, stride=rows), :] for p in pieces], axis=1)

    for x in range(rows):
        old[x + 2] = gather(state, x) if first else state[x]
        hx[x + 1] = 0.5 * gather(cx, x)
        hy[x + 1] = 0.5 * gather(cy, x)
    for h in range(2):
        old[h] = before[h]
        old[rows + 2 + h] = after[h]
    hx[0], hy[0] = 0.5 * far_before[2], 0.5 * far_before[3]
    hx[rows + 1], hy[rows + 1] = 0.5 * far_after[2], 0.5 * far_after[3]
    for x in range(rows + 2):
        new = stepped(old[x + 1], old[x + 2], old[x], hx[x], hy[x])
        if x == 0:
            new = new * inside[0]
        if x == rows + 1:
            new = new * inside[1]
        mid[x] = new
    for x in range(rows):
        new = stepped(mid[x + 1], mid[x + 2], mid[x], hx[x + 1], hy[x + 1])
        if not last:
            out[x] = new
            if x < 2:
                high[x] = new
            if x >= rows - 2:
                low[x - rows + 2] = new
        else:
            for i in range(parts):
                flat[i, pl.ds(x, 8, stride=rows), :] = new[:, at(i)]
    if last:
        for i in range(parts):
            out[:, at(i)] = target[i][...] - flat[i] if target else flat[i]


def mid_kernel(block_ref, spectrum_ref, rh, rl, rth, rtl, ch, cl, cth, ctl, out_ref):
    count, _, rows, cols = block_ref.shape
    field = block_ref[...].reshape(count * rows, cols)
    along_y = dot3(split(field), (cth[...], ctl[...]))
    full = dot3((rh[...], rl[...]), split(along_y)) * spectrum_ref[...]
    back = dot3((rth[...], rtl[...]), split(full))
    out_ref[...] = dot3(split(back), (ch[...], cl[...])).reshape(count, 1, rows, cols)


def mix_kernel(rows, field_ref, vh_ref, vl_ref, *refs):
    out_ref = refs[-1]
    levels = vh_ref.shape[1]
    factor = (vh_ref[...], vl_ref[...])
    for x in range(rows):
        field = field_ref[pl.ds(x, levels, stride=rows), :]
        out_ref[pl.ds(x, levels, stride=rows), :] = dot3(factor, split(field))


def params(**more):
    return pltpu.CompilerParams(vmem_limit_bytes=56 << 20, **more)


def chunk_of(cuts, levels, bricks):
    ends = [max(1, round(c * (levels // bricks) / 8)) * bricks for c in cuts]
    return [(a, b) for a, b in zip([0] + ends[:-1], ends) if b > a]


def jobs_of(subs, levels, bricks):
    jobs = []
    for target in range(subs - 1, 0, -1):
        cuts = CUTS_LAST if target == subs - 1 else CUTS_FIRST
        jobs += [(f"s{target}l{a}", target - 1, target, a, b) for a, b in chunk_of(cuts, levels, bricks)]
    return jobs + [(f"s0l{a}", subs - 1, None, a, b) for a, b in chunk_of(CUTS_FIRST, levels, bricks)]


def on_device(increments, courant_x, courant_y, spectrum, vertical):
    subs, levels, rows, cols = increments.shape
    bricks, groups = lax.axis_size("brick"), lax.axis_size("sub")
    brick = lax.axis_index("brick")
    f32 = jnp.float32

    def neighbour(value, by, part_of_end):
        pairs = []
        for g in range(groups - 1 if part_of_end else groups):
            pairs += [(g * bricks + i, g * bricks + i + by) for i in range(bricks) if 0 <= i + by < bricks]
        return lax.ppermute(value, ("sub", "brick"), pairs)

    def next_sub(value):
        return lax.ppermute(value, "sub", [(i, i + 1) for i in range(groups - 1)])

    row_table, col_table = dct_table(rows * bricks), dct_table(cols)
    tables = (*halves(row_table), *halves(row_table.T), *halves(col_table), *halves(col_table.T))

    def cost(values, passes):
        return pl.CostEstimate(flops=20 * values * passes, bytes_accessed=16 * values * passes, transcendentals=0)

    parts = cols // LANES
    flat_all = [a.reshape(-1, cols) for a in (increments, courant_x, courant_y)]
    inside = jnp.stack([jnp.where(brick > 0, 1.0, 0.0), jnp.where(brick < bricks - 1, 1.0, 0.0)]).astype(f32)

    def pieces(array, sub, start):
        specs = [
            pl.BlockSpec((8 * rows, LANES), lambda i, j=j: ((sub * levels + start) // 8 + i, j)) for j in range(parts)
        ]
        return [array] * parts, specs

    def edges(sub, start, stop):
        size = 16
        block = lambda at: pl.BlockSpec((size, 8, cols), lambda i: ((sub * levels + start) // size + i, at, 0))
        arrays = [a.reshape(-1, rows, cols) for a in (increments, courant_x, courant_y)]
        return pl.pallas_call(
            edge_kernel,
            grid=((stop - start) // size,),
            in_specs=[block(rows // 8 - 1)] * 3 + [block(0)] * 3,
            out_specs=[pl.BlockSpec((4, size, cols), lambda i: (0, i, 0))] * 2,
            out_shape=[jax.ShapeDtypeStruct((4, stop - start, cols), f32)] * 2,
            compiler_params=params(),
            cost_estimate=pl.CostEstimate(flops=0, bytes_accessed=200 * (stop - start) * cols, transcendentals=0),
            name="edge",
        )(*arrays, *arrays)

    def tangent(number, sub, start, stop, state, halo, far, target):
        span = stop - start
        first = number == 0
        last = None if first else ("end" if target is None else "jump")
        slab = pl.BlockSpec((rows, 8, cols), lambda i: (0, i, 0))
        inputs, specs = [inside], [pl.BlockSpec(memory_space=pltpu.SMEM)]

        def add(more, with_specs):
            inputs.extend(more)
            specs.extend(with_specs)

        if first:
            add(*pieces(flat_all[0], sub, start))
        else:
            add([state], [slab])
        add(*pieces(flat_all[1], sub, start))
        add(*pieces(flat_all[2], sub, start))
        for pair in (halo,) if first else (halo, far):
            add(pair, [pl.BlockSpec((pair[0].shape[0], 8, cols), lambda i: (0, i, 0))] * 2)
        if last == "jump":
            add(*pieces(flat_all[0], target, start))
        if first:
            pair = pl.BlockSpec((2, 8, cols), lambda i: (0, i, 0))
            out, out_spec = [(rows, span, cols)] + [(2, span, cols)] * 2, [slab, pair, pair]
        else:
            out, out_spec = [(span * rows, cols)], [pl.BlockSpec((8 * rows, cols), lambda i: (i, 0))]
        return pl.pallas_call(
            functools.partial(tangent_kernel, rows, parts, first, last),
            grid=(span // 8,),
            in_specs=specs,
            out_specs=out_spec,
            out_shape=[jax.ShapeDtypeStruct(o, f32) for o in out],
            scratch_shapes=[
                pltpu.VMEM((rows + 4, 8, cols), f32),
                pltpu.VMEM((rows + 2, 8, cols), f32),
                pltpu.VMEM((rows + 2, 8, cols), f32),
                pltpu.VMEM((rows + 2, 8, cols), f32),
                pltpu.VMEM((parts, 8 * rows, LANES), f32),
            ],
            compiler_params=params(),
            cost_estimate=cost(span * rows * cols, 2),
            name="tangent",
        )(*inputs)

    def advance(sub, target, start, stop):
        low, high = edges(sub, start, stop)
        last = sub == subs - 1
        far = neighbour(low, 1, last), neighbour(high, -1, last)
        state, low, high = tangent(0, sub, start, stop, None, far, far, None)
        near = neighbour(low, 1, last), neighbour(high, -1, last)
        (moved,) = tangent(1, sub, start, stop, state, near, far, target)
        moved = moved.reshape(-1, rows, cols)
        if target is None:
            moved = increments[0, start:stop] - next_sub(moved)
        return moved

    def spread(value):
        return lax.all_to_all(value, "brick", split_axis=0, concat_axis=0, tiled=True)

    def middle(block, done, offset, total):
        share = block.shape[0] // bricks
        block = block.reshape(bricks, share, rows, cols)
        fixed = [pl.BlockSpec(t.shape, lambda i: (0, 0), pipeline_mode=pl.Buffered(1)) for t in (spectrum, *tables)]
        piece = pl.BlockSpec((bricks, 1, rows, cols), lambda i: (0, i, 0, 0))
        flops = 12 * share * bricks * rows * cols * (cols + bricks * rows)
        inputs = [block, spectrum, *tables]
        specs = [piece] + fixed
        kernel, alias = mid_kernel, {}
        if done is not None:
            alias = {len(inputs): 0}
            inputs.append(done)
            specs.append(pl.BlockSpec(memory_space=pl.ANY))
            kernel = lambda *refs: mid_kernel(*refs[:-2], refs[-1])
        return pl.pallas_call(
            kernel,
            grid=(share,),
            in_specs=specs,
            out_specs=pl.BlockSpec((bricks, 1, rows, cols), lambda i: (0, i + offset, 0, 0)),
            out_shape=jax.ShapeDtypeStruct((bricks, total, rows, cols), f32),
            input_output_aliases=alias,
            compiler_params=params(),
            cost_estimate=pl.CostEstimate(flops=flops, bytes_accessed=8 * block.size, transcendentals=0),
            name="middle",
        )(*inputs)

    def mix(field, sub, factor, old):
        field = field.reshape(levels * rows, cols)
        inputs = [field, *factor]
        whole = pl.BlockSpec((levels, levels), lambda i: (0, 0))
        specs = [pl.BlockSpec((levels * rows, LANES), lambda i: (0, i)), whole, whole]
        kernel, alias = functools.partial(mix_kernel, rows), {}
        if old is not None:
            inputs.append(old)
            specs.append(pl.BlockSpec(memory_space=pl.ANY))
            alias = {3: 0}
        return pl.pallas_call(
            kernel,
            grid=(parts,),
            in_specs=specs,
            out_specs=pl.BlockSpec((levels * rows, LANES), lambda i: (sub, i)),
            out_shape=jax.ShapeDtypeStruct((subs * levels * rows, cols), f32),
            input_output_aliases=alias,
            compiler_params=params(),
            cost_estimate=pl.CostEstimate(
                flops=6 * levels * levels * rows * cols, bytes_accessed=8 * levels * rows * cols, transcendentals=0
            ),
            name="mix",
        )(*inputs)

    out = None
    work = {}
    for name, sub, target, start, stop in jobs_of(subs, levels, bricks):
        moved = advance(sub, target, start, stop)
        block = spread(moved)
        work.setdefault(0 if target is None else target, []).append((name, start, stop, block))
    returned = []
    for sub, group in work.items():
        done, offset, columns = None, 0, []
        for name, a, b, block in group:
            share = (b - a) // bricks
            done = middle(block, done, offset, levels // bricks)
            offset += share
            columns.append(vertical[:, a:b].reshape(levels, bricks, share))
        factor = jnp.concatenate(columns, axis=2).reshape(levels, levels)
        returned.append((sub, halves(factor), spread(done)))
    for sub, factor, part in returned:
        out = mix(part, sub, factor, out)
    return out.reshape(increments.shape)


def solution(mesh):
    spec = P("sub", None, "brick", None)
    return jax.shard_map(
        on_device, mesh=mesh, in_specs=(spec, spec, spec, P(), P()), out_specs=spec, check_vma=False
    )
```

```python
import functools

import jax
import jax.numpy as jnp
from jax import lax
from jax.experimental import pallas as pl
from jax.experimental.pallas import tpu as pltpu
from jax.sharding import PartitionSpec as P


LANES = 128
DIFFUSION = 0.2
CUTS_LAST = (4, 8)
CUTS_FIRST = (8,)
HOLD = 0


def dct_table(count):
    freq = jnp.arange(count, dtype=jnp.float32)[:, None]
    cells = jnp.arange(count, dtype=jnp.float32)[None, :]
    table = jnp.cos(jnp.pi * (cells + 0.5) * freq / count) * jnp.sqrt(jnp.float32(2.0) / count)
    first = jnp.where(jnp.arange(count)[:, None] == 0, jnp.sqrt(jnp.float32(0.5)), jnp.float32(1.0))
    return table * first


def halves(table):
    high = lax.reduce_precision(table, 8, 7)
    return high.astype(jnp.bfloat16), (table - high).astype(jnp.bfloat16)


def split(value):
    high = value.astype(jnp.bfloat16)
    return high, (value - high.astype(jnp.float32)).astype(jnp.bfloat16)


def dot3(left, right):
    dot = functools.partial(jnp.dot, preferred_element_type=jnp.float32)
    return dot(left[0], right[0]) + (dot(left[0], right[1]) + dot(left[1], right[0]))


def beside(center):
    cols = center.shape[1]
    lane = lax.broadcasted_iota(jnp.int32, center.shape, 1)
    east = jnp.where(lane == cols - 1, 0.0, pltpu.roll(center, cols - 1, 1))
    west = jnp.where(lane == 0, 0.0, pltpu.roll(center, 1, 1))
    return east, west


def stepped(center, north, south, half_x, half_y):
    east, west = beside(center)
    total = (north + south) + (east + west) + center
    return DIFFUSION * total - half_x * (north - south) - half_y * (east - west)


def offered(center, inner, half_x, half_y, sign):
    east, west = beside(center)
    return DIFFUSION * (center + (east + west) + inner) + sign * half_x * inner - half_y * (east - west)


def edge_kernel(inc_b, cx_b, cy_b, inc_t, cx_t, cy_t, low, high):
    half_x, half_y = 0.5 * cx_b[:, 7, :], 0.5 * cy_b[:, 7, :]
    low[0] = inc_b[:, 7, :]
    low[1] = offered(inc_b[:, 7, :], inc_b[:, 6, :], half_x, half_y, 1.0)
    low[2] = DIFFUSION - half_x
    half_x, half_y = 0.5 * cx_t[:, 0, :], 0.5 * cy_t[:, 0, :]
    high[0] = inc_t[:, 0, :]
    high[1] = offered(inc_t[:, 0, :], inc_t[:, 1, :], half_x, half_y, -1.0)
    high[2] = DIFFUSION + half_x


def tangent_kernel(rows, parts, first, last, hold, *refs):
    refs = list(refs)

    def take(count):
        taken = refs[:count]
        del refs[:count]
        return taken

    held = take(1) if hold else None
    state = take(parts) if first else take(1)[0]
    cx, cy = take(parts), take(parts)
    before, after = take(2)
    if first:
        share_before, share_after = before.at[2], after.at[2]
    else:
        share_before, share_after = (r.at[0] for r in take(2))
    target = take(parts) if last == "jump" else None
    (out,) = take(1)
    low, high = (None, None) if last else take(2)
    old, mid, hx, hy, flat = refs
    at = lambda i: slice(i * LANES, (i + 1) * LANES)

    def gather(pieces, x):
        return jnp.concatenate([p[pl.ds(x, 8, stride=rows), :] for p in pieces], axis=1)

    if hold:

        @pl.when(pl.program_id(0) == 0)
        def _():
            def more(_, carry):
                mid[0] = mid[0] + 1.0
                return carry

            lax.fori_loop(0, held[0][0], more, 0)

    for x in range(rows):
        old[x + 1] = gather(state, x) if first else state[x]
        hx[x] = 0.5 * gather(cx, x)
        hy[x] = 0.5 * gather(cy, x)
    old[0] = before[0]
    old[rows + 1] = after[0]
    mid[0] = before[1] + share_before[...] * old[1]
    mid[rows + 1] = after[1] + share_after[...] * old[rows]
    for x in range(rows):
        mid[x + 1] = stepped(old[x + 1], old[x + 2], old[x], hx[x], hy[x])
    for x in range(rows):
        new = stepped(mid[x + 1], mid[x + 2], mid[x], hx[x], hy[x])
        if not last:
            out[x] = new
        else:
            for i in range(parts):
                flat[i, pl.ds(x, 8, stride=rows), :] = new[:, at(i)]
    if last:
        for i in range(parts):
            out[:, at(i)] = target[i][...] - flat[i] if target else flat[i]
    else:
        low[0] = out[rows - 1]
        low[1] = offered(out[rows - 1], out[rows - 2], hx[rows - 1], hy[rows - 1], 1.0)
        high[0] = out[0]
        high[1] = offered(out[0], out[1], hx[0], hy[0], -1.0)


def mid_kernel(block_ref, spectrum_ref, rh, rl, rth, rtl, ch, cl, cth, ctl, out_ref):
    count, _, rows, cols = block_ref.shape
    field = block_ref[...].reshape(count * rows, cols)
    along_y = dot3(split(field), (cth[...], ctl[...]))
    full = dot3((rh[...], rl[...]), split(along_y)) * spectrum_ref[...]
    back = dot3((rth[...], rtl[...]), split(full))
    out_ref[...] = dot3(split(back), (ch[...], cl[...])).reshape(count, 1, rows, cols)


def mix_kernel(rows, field_ref, vh_ref, vl_ref, *refs):
    out_ref = refs[-1]
    levels = vh_ref.shape[1]
    factor = (vh_ref[...], vl_ref[...])
    for x in range(rows):
        field = field_ref[pl.ds(x, levels, stride=rows), :]
        out_ref[pl.ds(x, levels, stride=rows), :] = dot3(factor, split(field))


def params(**more):
    return pltpu.CompilerParams(vmem_limit_bytes=56 << 20, **more)


def chunk_of(cuts, levels, bricks):
    ends = [max(1, round(c * (levels // bricks) / 8)) * bricks for c in cuts]
    return [(a, b) for a, b in zip([0] + ends[:-1], ends) if b > a]


def jobs_of(subs, levels, bricks):
    jobs = []
    for target in range(subs - 1, 0, -1):
        cuts = CUTS_LAST if target == subs - 1 else CUTS_FIRST
        jobs += [(f"s{target}l{a}", target - 1, target, a, b) for a, b in chunk_of(cuts, levels, bricks)]
    return jobs + [(f"s0l{a}", subs - 1, None, a, b) for a, b in chunk_of(CUTS_FIRST, levels, bricks)]


def on_device(increments, courant_x, courant_y, spectrum, vertical):
    subs, levels, rows, cols = increments.shape
    bricks, groups = lax.axis_size("brick"), lax.axis_size("sub")
    f32 = jnp.float32

    def neighbour(value, by, part_of_end):
        pairs = []
        for g in range(groups - 1 if part_of_end else groups):
            pairs += [(g * bricks + i, g * bricks + i + by) for i in range(bricks) if 0 <= i + by < bricks]
        return lax.ppermute(value, ("sub", "brick"), pairs)

    def next_sub(value):
        return lax.ppermute(value, "sub", [(i, i + 1) for i in range(groups - 1)])

    row_table, col_table = dct_table(rows * bricks), dct_table(cols)
    tables = (*halves(row_table), *halves(row_table.T), *halves(col_table), *halves(col_table.T))

    def cost(values, passes):
        return pl.CostEstimate(flops=20 * values * passes, bytes_accessed=16 * values * passes, transcendentals=0)

    parts = cols // LANES
    flat_all = [a.reshape(-1, cols) for a in (increments, courant_x, courant_y)]
    late = (lax.axis_index("sub") % 2 * HOLD).astype(jnp.int32).reshape(1)

    def pieces(array, sub, start):
        specs = [
            pl.BlockSpec((8 * rows, LANES), lambda i, j=j: ((sub * levels + start) // 8 + i, j)) for j in range(parts)
        ]
        return [array] * parts, specs

    def edges(sub, start, stop):
        size = 16
        block = lambda at: pl.BlockSpec((size, 8, cols), lambda i: ((sub * levels + start) // size + i, at, 0))
        arrays = [a.reshape(-1, rows, cols) for a in (increments, courant_x, courant_y)]
        return pl.pallas_call(
            edge_kernel,
            grid=((stop - start) // size,),
            in_specs=[block(rows // 8 - 1)] * 3 + [block(0)] * 3,
            out_specs=[pl.BlockSpec((3, size, cols), lambda i: (0, i, 0))] * 2,
            out_shape=[jax.ShapeDtypeStruct((3, stop - start, cols), f32)] * 2,
            compiler_params=params(),
            cost_estimate=pl.CostEstimate(flops=0, bytes_accessed=200 * (stop - start) * cols, transcendentals=0),
            name="edge",
        )(*arrays, *arrays)

    def tangent(number, sub, start, stop, state, halo, far, target, hold):
        span = stop - start
        first = number == 0
        last = None if first else ("end" if target is None else "jump")
        slab = pl.BlockSpec((rows, 8, cols), lambda i: (0, i, 0))
        inputs, specs = ([late], [pl.BlockSpec(memory_space=pltpu.SMEM)]) if hold else ([], [])

        def add(more, with_specs):
            inputs.extend(more)
            specs.extend(with_specs)

        if first:
            add(*pieces(flat_all[0], sub, start))
        else:
            add([state], [slab])
        add(*pieces(flat_all[1], sub, start))
        add(*pieces(flat_all[2], sub, start))
        add(halo, [pl.BlockSpec((halo[0].shape[0], 8, cols), lambda i: (0, i, 0))] * 2)
        if not first:
            add(far, [pl.BlockSpec((1, 8, cols), lambda i: (2, i, 0))] * 2)
        if last == "jump":
            add(*pieces(flat_all[0], target, start))
        if first:
            pair = pl.BlockSpec((2, 8, cols), lambda i: (0, i, 0))
            out, out_spec = [(rows, span, cols)] + [(2, span, cols)] * 2, [slab, pair, pair]
        else:
            out, out_spec = [(span * rows, cols)], [pl.BlockSpec((8 * rows, cols), lambda i: (i, 0))]
        return pl.pallas_call(
            functools.partial(tangent_kernel, rows, parts, first, last, hold),
            grid=(span // 8,),
            in_specs=specs,
            out_specs=out_spec,
            out_shape=[jax.ShapeDtypeStruct(o, f32) for o in out],
            scratch_shapes=[
                pltpu.VMEM((rows + 2, 8, cols), f32),
                pltpu.VMEM((rows + 2, 8, cols), f32),
                pltpu.VMEM((rows, 8, cols), f32),
                pltpu.VMEM((rows, 8, cols), f32),
                pltpu.VMEM((parts, 8 * rows, LANES), f32),
            ],
            compiler_params=params(),
            cost_estimate=cost(span * rows * cols, 2),
            name="tangent",
        )(*inputs)

    def advance(sub, target, start, stop, hold):
        low, high = edges(sub, start, stop)
        last = sub == subs - 1
        far = neighbour(low, 1, last), neighbour(high, -1, last)
        state, low, high = tangent(0, sub, start, stop, None, far, far, None, False)
        near = neighbour(low, 1, last), neighbour(high, -1, last)
        (moved,) = tangent(1, sub, start, stop, state, near, far, target, HOLD > 0 and hold)
        moved = moved.reshape(-1, rows, cols)
        if target is None:
            moved = increments[0, start:stop] - next_sub(moved)
        return moved

    def spread(value):
        return lax.all_to_all(value, "brick", split_axis=0, concat_axis=0, tiled=True)

    def middle(block, done, offset, total):
        share = block.shape[0] // bricks
        block = block.reshape(bricks, share, rows, cols)
        fixed = [pl.BlockSpec(t.shape, lambda i: (0, 0), pipeline_mode=pl.Buffered(1)) for t in (spectrum, *tables)]
        piece = pl.BlockSpec((bricks, 1, rows, cols), lambda i: (0, i, 0, 0))
        flops = 12 * share * bricks * rows * cols * (cols + bricks * rows)
        inputs = [block, spectrum, *tables]
        specs = [piece] + fixed
        kernel, alias = mid_kernel, {}
        if done is not None:
            alias = {len(inputs): 0}
            inputs.append(done)
            specs.append(pl.BlockSpec(memory_space=pl.ANY))
            kernel = lambda *refs: mid_kernel(*refs[:-2], refs[-1])
        return pl.pallas_call(
            kernel,
            grid=(share,),
            in_specs=specs,
            out_specs=pl.BlockSpec((bricks, 1, rows, cols), lambda i: (0, i + offset, 0, 0)),
            out_shape=jax.ShapeDtypeStruct((bricks, total, rows, cols), f32),
            input_output_aliases=alias,
            compiler_params=params(),
            cost_estimate=pl.CostEstimate(flops=flops, bytes_accessed=8 * block.size, transcendentals=0),
            name="middle",
        )(*inputs)

    def mix(field, sub, factor, old):
        field = field.reshape(levels * rows, cols)
        inputs = [field, *factor]
        whole = pl.BlockSpec((levels, levels), lambda i: (0, 0))
        specs = [pl.BlockSpec((levels * rows, LANES), lambda i: (0, i)), whole, whole]
        kernel, alias = functools.partial(mix_kernel, rows), {}
        if old is not None:
            inputs.append(old)
            specs.append(pl.BlockSpec(memory_space=pl.ANY))
            alias = {3: 0}
        return pl.pallas_call(
            kernel,
            grid=(parts,),
            in_specs=specs,
            out_specs=pl.BlockSpec((levels * rows, LANES), lambda i: (sub, i)),
            out_shape=jax.ShapeDtypeStruct((subs * levels * rows, cols), f32),
            input_output_aliases=alias,
            compiler_params=params(),
            cost_estimate=pl.CostEstimate(
                flops=6 * levels * levels * rows * cols, bytes_accessed=8 * levels * rows * cols, transcendentals=0
            ),
            name="mix",
        )(*inputs)

    out = None
    work = {}
    for name, sub, target, start, stop in jobs_of(subs, levels, bricks):
        moved = advance(sub, target, start, stop, not work)
        block = spread(moved)
        work.setdefault(0 if target is None else target, []).append((name, start, stop, block))
    returned = []
    for sub, group in work.items():
        done, offset, columns = None, 0, []
        for name, a, b, block in group:
            share = (b - a) // bricks
            done = middle(block, done, offset, levels // bricks)
            offset += share
            columns.append(vertical[:, a:b].reshape(levels, bricks, share))
        factor = jnp.concatenate(columns, axis=2).reshape(levels, levels)
        returned.append((sub, halves(factor), spread(done)))
    for sub, factor, part in returned:
        out = mix(part, sub, factor, out)
    return out.reshape(increments.shape)


def solution(mesh):
    spec = P("sub", None, "brick", None)
    return jax.shard_map(
        on_device, mesh=mesh, in_specs=(spec, spec, spec, P(), P()), out_specs=spec, check_vma=False
    )
```

```python
import functools

import jax
import jax.numpy as jnp
from jax import lax
from jax.experimental import pallas as pl
from jax.experimental.pallas import tpu as pltpu
from jax.sharding import PartitionSpec as P


LANES = 128
DIFFUSION = 0.2
CUTS_LAST = (4, 8)
CUTS_FIRST = (8,)
STACK = 4


def dct_table(count):
    freq = jnp.arange(count, dtype=jnp.float32)[:, None]
    cells = jnp.arange(count, dtype=jnp.float32)[None, :]
    table = jnp.cos(jnp.pi * (cells + 0.5) * freq / count) * jnp.sqrt(jnp.float32(2.0) / count)
    first = jnp.where(jnp.arange(count)[:, None] == 0, jnp.sqrt(jnp.float32(0.5)), jnp.float32(1.0))
    return table * first


def halves(table):
    high = lax.reduce_precision(table, 8, 7)
    return high.astype(jnp.bfloat16), (table - high).astype(jnp.bfloat16)


def split(value):
    high = value.astype(jnp.bfloat16)
    return high, (value - high.astype(jnp.float32)).astype(jnp.bfloat16)


def dot3(left, right):
    dot = functools.partial(jnp.dot, preferred_element_type=jnp.float32)
    return dot(left[0], right[0]) + (dot(left[0], right[1]) + dot(left[1], right[0]))


def beside(center):
    cols = center.shape[1]
    lane = lax.broadcasted_iota(jnp.int32, center.shape, 1)
    east = jnp.where(lane == cols - 1, 0.0, pltpu.roll(center, cols - 1, 1))
    west = jnp.where(lane == 0, 0.0, pltpu.roll(center, 1, 1))
    return east, west


def stepped(center, north, south, half_x, half_y):
    east, west = beside(center)
    total = (north + south) + (east + west) + center
    return DIFFUSION * total - half_x * (north - south) - half_y * (east - west)


def offered(center, inner, half_x, half_y, sign):
    east, west = beside(center)
    return DIFFUSION * (center + (east + west) + inner) + sign * half_x * inner - half_y * (east - west)


def edge_kernel(inc_b, cx_b, cy_b, inc_t, cx_t, cy_t, low, high):
    half_x, half_y = 0.5 * cx_b[:, 7, :], 0.5 * cy_b[:, 7, :]
    low[0] = inc_b[:, 7, :]
    low[1] = offered(inc_b[:, 7, :], inc_b[:, 6, :], half_x, half_y, 1.0)
    low[2] = DIFFUSION - half_x
    half_x, half_y = 0.5 * cx_t[:, 0, :], 0.5 * cy_t[:, 0, :]
    high[0] = inc_t[:, 0, :]
    high[1] = offered(inc_t[:, 0, :], inc_t[:, 1, :], half_x, half_y, -1.0)
    high[2] = DIFFUSION + half_x


def tangent_kernel(rows, parts, first, last, *refs):
    refs = list(refs)

    def take(count):
        taken = refs[:count]
        del refs[:count]
        return taken

    state = take(parts) if first else take(1)[0]
    cx, cy = take(parts), take(parts)
    before, after = take(2)
    if first:
        share_before, share_after = before.at[2], after.at[2]
    else:
        share_before, share_after = (r.at[0] for r in take(2))
    target = take(parts) if last == "jump" else None
    (out,) = take(1)
    low, high = (None, None) if last else take(2)
    old, mid, hx, hy, flat = refs
    at = lambda i: slice(i * LANES, (i + 1) * LANES)
    stack = out.shape[0] // (8 * rows) if last else out.shape[1] // 8

    for g in range(stack):
        group = pl.ds(8 * g, 8)
        every = lambda x: pl.ds(8 * g * rows + x, 8, stride=rows)

        def gather(pieces, x):
            return jnp.concatenate([p[every(x), :] for p in pieces], axis=1)

        for x in range(rows):
            old[x + 1] = gather(state, x) if first else state[x, group]
            hx[x] = 0.5 * gather(cx, x)
            hy[x] = 0.5 * gather(cy, x)
        old[0] = before[0, group]
        old[rows + 1] = after[0, group]
        mid[0] = before[1, group] + share_before[group] * old[1]
        mid[rows + 1] = after[1, group] + share_after[group] * old[rows]
        for x in range(rows):
            mid[x + 1] = stepped(old[x + 1], old[x + 2], old[x], hx[x], hy[x])
        for x in range(rows):
            new = stepped(mid[x + 1], mid[x + 2], mid[x], hx[x], hy[x])
            if not last:
                out[x, group] = new
            else:
                for i in range(parts):
                    flat[i, pl.ds(x, 8, stride=rows), :] = new[:, at(i)]
        if last:
            block = pl.ds(8 * g * rows, 8 * rows)
            for i in range(parts):
                out[block, at(i)] = target[i][block, :] - flat[i] if target else flat[i]
        else:
            final, first_row = out[rows - 1, group], out[0, group]
            low[0, group] = final
            low[1, group] = offered(final, out[rows - 2, group], hx[rows - 1], hy[rows - 1], 1.0)
            high[0, group] = first_row
            high[1, group] = offered(first_row, out[1, group], hx[0], hy[0], -1.0)


def mid_kernel(block_ref, spectrum_ref, rh, rl, rth, rtl, ch, cl, cth, ctl, out_ref):
    count, _, rows, cols = block_ref.shape
    field = block_ref[...].reshape(count * rows, cols)
    along_y = dot3(split(field), (cth[...], ctl[...]))
    full = dot3((rh[...], rl[...]), split(along_y)) * spectrum_ref[...]
    back = dot3((rth[...], rtl[...]), split(full))
    out_ref[...] = dot3(split(back), (ch[...], cl[...])).reshape(count, 1, rows, cols)


def mix_kernel(rows, field_ref, vh_ref, vl_ref, *refs):
    out_ref = refs[-1]
    levels = vh_ref.shape[1]
    factor = (vh_ref[...], vl_ref[...])
    for x in range(rows):
        field = field_ref[pl.ds(x, levels, stride=rows), :]
        out_ref[pl.ds(x, levels, stride=rows), :] = dot3(factor, split(field))


def params(**more):
    return pltpu.CompilerParams(vmem_limit_bytes=56 << 20, **more)


def chunk_of(cuts, levels, bricks):
    ends = [max(1, round(c * (levels // bricks) / 8)) * bricks for c in cuts]
    return [(a, b) for a, b in zip([0] + ends[:-1], ends) if b > a]


def jobs_of(subs, levels, bricks):
    jobs = []
    for target in range(subs - 1, 0, -1):
        cuts = CUTS_LAST if target == subs - 1 else CUTS_FIRST
        jobs += [(f"s{target}l{a}", target - 1, target, a, b) for a, b in chunk_of(cuts, levels, bricks)]
    return jobs + [(f"s0l{a}", subs - 1, None, a, b) for a, b in chunk_of(CUTS_FIRST, levels, bricks)]


def on_device(increments, courant_x, courant_y, spectrum, vertical):
    subs, levels, rows, cols = increments.shape
    bricks, groups = lax.axis_size("brick"), lax.axis_size("sub")
    f32 = jnp.float32

    def neighbour(value, by, part_of_end):
        pairs = []
        for g in range(groups - 1 if part_of_end else groups):
            pairs += [(g * bricks + i, g * bricks + i + by) for i in range(bricks) if 0 <= i + by < bricks]
        return lax.ppermute(value, ("sub", "brick"), pairs)

    def next_sub(value):
        return lax.ppermute(value, "sub", [(i, i + 1) for i in range(groups - 1)])

    row_table, col_table = dct_table(rows * bricks), dct_table(cols)
    tables = (*halves(row_table), *halves(row_table.T), *halves(col_table), *halves(col_table.T))

    def cost(values, passes):
        return pl.CostEstimate(flops=20 * values * passes, bytes_accessed=16 * values * passes, transcendentals=0)

    parts = cols // LANES
    flat_all = [a.reshape(-1, cols) for a in (increments, courant_x, courant_y)]

    def pieces(array, sub, start):
        specs = [
            pl.BlockSpec((8 * STACK * rows, LANES), lambda i, j=j: ((sub * levels + start) // (8 * STACK) + i, j))
            for j in range(parts)
        ]
        return [array] * parts, specs

    def edges(sub, start, stop):
        size = 16
        block = lambda at: pl.BlockSpec((size, 8, cols), lambda i: ((sub * levels + start) // size + i, at, 0))
        arrays = [a.reshape(-1, rows, cols) for a in (increments, courant_x, courant_y)]
        return pl.pallas_call(
            edge_kernel,
            grid=((stop - start) // size,),
            in_specs=[block(rows // 8 - 1)] * 3 + [block(0)] * 3,
            out_specs=[pl.BlockSpec((3, size, cols), lambda i: (0, i, 0))] * 2,
            out_shape=[jax.ShapeDtypeStruct((3, stop - start, cols), f32)] * 2,
            compiler_params=params(),
            cost_estimate=pl.CostEstimate(flops=0, bytes_accessed=200 * (stop - start) * cols, transcendentals=0),
            name="edge",
        )(*arrays, *arrays)

    def tangent(number, sub, start, stop, state, halo, far, target):
        span = stop - start
        first = number == 0
        last = None if first else ("end" if target is None else "jump")
        slab = pl.BlockSpec((rows, 8 * STACK, cols), lambda i: (0, i, 0))
        inputs, specs = [], []

        def add(more, with_specs):
            inputs.extend(more)
            specs.extend(with_specs)

        if first:
            add(*pieces(flat_all[0], sub, start))
        else:
            add([state], [slab])
        add(*pieces(flat_all[1], sub, start))
        add(*pieces(flat_all[2], sub, start))
        add(halo, [pl.BlockSpec((halo[0].shape[0], 8 * STACK, cols), lambda i: (0, i, 0))] * 2)
        if not first:
            add(far, [pl.BlockSpec((1, 8 * STACK, cols), lambda i: (2, i, 0))] * 2)
        if last == "jump":
            add(*pieces(flat_all[0], target, start))
        if first:
            pair = pl.BlockSpec((2, 8 * STACK, cols), lambda i: (0, i, 0))
            out, out_spec = [(rows, span, cols)] + [(2, span, cols)] * 2, [slab, pair, pair]
        else:
            out, out_spec = [(span * rows, cols)], [pl.BlockSpec((8 * STACK * rows, cols), lambda i: (i, 0))]
        return pl.pallas_call(
            functools.partial(tangent_kernel, rows, parts, first, last),
            grid=(span // (8 * STACK),),
            in_specs=specs,
            out_specs=out_spec,
            out_shape=[jax.ShapeDtypeStruct(o, f32) for o in out],
            scratch_shapes=[
                pltpu.VMEM((rows + 2, 8, cols), f32),
                pltpu.VMEM((rows + 2, 8, cols), f32),
                pltpu.VMEM((rows, 8, cols), f32),
                pltpu.VMEM((rows, 8, cols), f32),
                pltpu.VMEM((parts, 8 * rows, LANES), f32),
            ],
            compiler_params=params(),
            cost_estimate=cost(span * rows * cols, 2),
            name="tangent",
        )(*inputs)

    def advance(sub, target, start, stop):
        low, high = edges(sub, start, stop)
        last = sub == subs - 1
        far = neighbour(low, 1, last), neighbour(high, -1, last)
        state, low, high = tangent(0, sub, start, stop, None, far, far, None)
        near = neighbour(low, 1, last), neighbour(high, -1, last)
        (moved,) = tangent(1, sub, start, stop, state, near, far, target)
        moved = moved.reshape(-1, rows, cols)
        if target is None:
            moved = increments[0, start:stop] - next_sub(moved)
        return moved

    def spread(value):
        return lax.all_to_all(value, "brick", split_axis=0, concat_axis=0, tiled=True)

    def middle(block, done, offset, total):
        share = block.shape[0] // bricks
        block = block.reshape(bricks, share, rows, cols)
        fixed = [pl.BlockSpec(t.shape, lambda i: (0, 0), pipeline_mode=pl.Buffered(1)) for t in (spectrum, *tables)]
        piece = pl.BlockSpec((bricks, 1, rows, cols), lambda i: (0, i, 0, 0))
        flops = 12 * share * bricks * rows * cols * (cols + bricks * rows)
        inputs = [block, spectrum, *tables]
        specs = [piece] + fixed
        kernel, alias = mid_kernel, {}
        if done is not None:
            alias = {len(inputs): 0}
            inputs.append(done)
            specs.append(pl.BlockSpec(memory_space=pl.ANY))
            kernel = lambda *refs: mid_kernel(*refs[:-2], refs[-1])
        return pl.pallas_call(
            kernel,
            grid=(share,),
            in_specs=specs,
            out_specs=pl.BlockSpec((bricks, 1, rows, cols), lambda i: (0, i + offset, 0, 0)),
            out_shape=jax.ShapeDtypeStruct((bricks, total, rows, cols), f32),
            input_output_aliases=alias,
            compiler_params=params(),
            cost_estimate=pl.CostEstimate(flops=flops, bytes_accessed=8 * block.size, transcendentals=0),
            name="middle",
        )(*inputs)

    def mix(field, sub, factor, old):
        field = field.reshape(levels * rows, cols)
        inputs = [field, *factor]
        whole = pl.BlockSpec((levels, levels), lambda i: (0, 0))
        specs = [pl.BlockSpec((levels * rows, LANES), lambda i: (0, i)), whole, whole]
        kernel, alias = functools.partial(mix_kernel, rows), {}
        if old is not None:
            inputs.append(old)
            specs.append(pl.BlockSpec(memory_space=pl.ANY))
            alias = {3: 0}
        return pl.pallas_call(
            kernel,
            grid=(parts,),
            in_specs=specs,
            out_specs=pl.BlockSpec((levels * rows, LANES), lambda i: (sub, i)),
            out_shape=jax.ShapeDtypeStruct((subs * levels * rows, cols), f32),
            input_output_aliases=alias,
            compiler_params=params(),
            cost_estimate=pl.CostEstimate(
                flops=6 * levels * levels * rows * cols, bytes_accessed=8 * levels * rows * cols, transcendentals=0
            ),
            name="mix",
        )(*inputs)

    out = None
    work = {}
    for name, sub, target, start, stop in jobs_of(subs, levels, bricks):
        moved = advance(sub, target, start, stop)
        block = spread(moved)
        work.setdefault(0 if target is None else target, []).append((name, start, stop, block))
    returned = []
    for sub, group in work.items():
        done, offset, columns = None, 0, []
        for name, a, b, block in group:
            share = (b - a) // bricks
            done = middle(block, done, offset, levels // bricks)
            offset += share
            columns.append(vertical[:, a:b].reshape(levels, bricks, share))
        factor = jnp.concatenate(columns, axis=2).reshape(levels, levels)
        returned.append((sub, halves(factor), spread(done)))
    for sub, factor, part in returned:
        out = mix(part, sub, factor, out)
    return out.reshape(increments.shape)


def solution(mesh):
    spec = P("sub", None, "brick", None)
    return jax.shard_map(
        on_device, mesh=mesh, in_specs=(spec, spec, spec, P(), P()), out_specs=spec, check_vma=False
    )
```

```python
import functools

import jax
import jax.numpy as jnp
from jax import lax
from jax.experimental import pallas as pl
from jax.experimental.pallas import tpu as pltpu
from jax.sharding import PartitionSpec as P


LANES = 128
DIFFUSION = 0.2
CUTS_LAST = (4, 8)
CUTS_FIRST = (8,)
STACK = 4


def dct_table(count):
    freq = jnp.arange(count, dtype=jnp.float32)[:, None]
    cells = jnp.arange(count, dtype=jnp.float32)[None, :]
    table = jnp.cos(jnp.pi * (cells + 0.5) * freq / count) * jnp.sqrt(jnp.float32(2.0) / count)
    first = jnp.where(jnp.arange(count)[:, None] == 0, jnp.sqrt(jnp.float32(0.5)), jnp.float32(1.0))
    return table * first


def halves(table):
    high = lax.reduce_precision(table, 8, 7)
    return high.astype(jnp.bfloat16), (table - high).astype(jnp.bfloat16)


def split(value):
    high = value.astype(jnp.bfloat16)
    return high, (value - high.astype(jnp.float32)).astype(jnp.bfloat16)


def dot3(left, right):
    dot = functools.partial(jnp.dot, preferred_element_type=jnp.float32)
    return dot(left[0], right[0]) + (dot(left[0], right[1]) + dot(left[1], right[0]))


def beside(center):
    cols = center.shape[1]
    lane = lax.broadcasted_iota(jnp.int32, center.shape, 1)
    east = jnp.where(lane == cols - 1, 0.0, pltpu.roll(center, cols - 1, 1))
    west = jnp.where(lane == 0, 0.0, pltpu.roll(center, 1, 1))
    return east, west


def stepped(center, north, south, half_x, half_y):
    east, west = beside(center)
    total = (north + south) + (east + west) + center
    return DIFFUSION * total - half_x * (north - south) - half_y * (east - west)


def offered(center, inner, half_x, half_y, sign):
    east, west = beside(center)
    return DIFFUSION * (center + (east + west) + inner) + sign * half_x * inner - half_y * (east - west)


def edge_kernel(inc_b, cx_b, cy_b, inc_t, cx_t, cy_t, low, high):
    half_x, half_y = 0.5 * cx_b[:, 7, :], 0.5 * cy_b[:, 7, :]
    low[0] = inc_b[:, 7, :]
    low[1] = offered(inc_b[:, 7, :], inc_b[:, 6, :], half_x, half_y, 1.0)
    low[2] = DIFFUSION - half_x
    half_x, half_y = 0.5 * cx_t[:, 0, :], 0.5 * cy_t[:, 0, :]
    high[0] = inc_t[:, 0, :]
    high[1] = offered(inc_t[:, 0, :], inc_t[:, 1, :], half_x, half_y, -1.0)
    high[2] = DIFFUSION + half_x


def tangent_kernel(rows, parts, first, last, *refs):
    refs = list(refs)

    def take(count):
        taken = refs[:count]
        del refs[:count]
        return taken

    state = take(parts) if first else take(1)[0]
    cx, cy = take(parts), take(parts)
    before, after = take(2)
    if first:
        share_before, share_after = before.at[2], after.at[2]
    else:
        share_before, share_after = (r.at[0] for r in take(2))
    target = take(parts) if last == "jump" else None
    (out,) = take(1)
    low, high = (None, None) if last else take(2)
    old, mid, hx, hy, flat = refs
    at = lambda i: slice(i * LANES, (i + 1) * LANES)
    stack = out.shape[0] // (8 * rows) if last else out.shape[1] // 8

    for g in range(stack):
        group = pl.ds(8 * g, 8)
        every = lambda x: pl.ds(8 * g * rows + x, 8, stride=rows)

        def gather(pieces, x):
            return jnp.concatenate([p[every(x), :] for p in pieces], axis=1)

        for x in range(rows):
            old[x + 1] = gather(state, x) if first else state[x, group]
            hx[x] = 0.5 * gather(cx, x)
            hy[x] = 0.5 * gather(cy, x)
        old[0] = before[0, group]
        old[rows + 1] = after[0, group]
        mid[0] = before[1, group] + share_before[group] * old[1]
        mid[rows + 1] = after[1, group] + share_after[group] * old[rows]
        for x in range(rows):
            mid[x + 1] = stepped(old[x + 1], old[x + 2], old[x], hx[x], hy[x])
        for x in range(rows):
            new = stepped(mid[x + 1], mid[x + 2], mid[x], hx[x], hy[x])
            if not last:
                out[x, group] = new
            else:
                for i in range(parts):
                    flat[i, pl.ds(x, 8, stride=rows), :] = new[:, at(i)]
        if last:
            block = pl.ds(8 * g * rows, 8 * rows)
            for i in range(parts):
                out[block, at(i)] = target[i][block, :] - flat[i] if target else flat[i]
        else:
            final, first_row = out[rows - 1, group], out[0, group]
            low[0, group] = final
            low[1, group] = offered(final, out[rows - 2, group], hx[rows - 1], hy[rows - 1], 1.0)
            high[0, group] = first_row
            high[1, group] = offered(first_row, out[1, group], hx[0], hy[0], -1.0)


def mid_kernel(block_ref, spectrum_ref, rh, rl, rth, rtl, ch, cl, cth, ctl, out_ref):
    count, _, rows, cols = block_ref.shape
    field = block_ref[...].reshape(count * rows, cols)
    along_y = dot3(split(field), (cth[...], ctl[...]))
    full = dot3((rh[...], rl[...]), split(along_y)) * spectrum_ref[...]
    back = dot3((rth[...], rtl[...]), split(full))
    out_ref[...] = dot3(split(back), (ch[...], cl[...])).reshape(count, 1, rows, cols)


def mix_kernel(field_ref, vh_ref, vl_ref, *refs):
    levels, height, lanes = field_ref.shape
    field, out = (r.reshape(levels * height, lanes) for r in (field_ref, refs[-1]))
    factor = (vh_ref[...], vl_ref[...])
    for x in range(height):
        own = pl.ds(x, levels, stride=height)
        out[own, :] = dot3(factor, split(field[own, :]))


def params(**more):
    return pltpu.CompilerParams(vmem_limit_bytes=56 << 20, **more)


def chunk_of(cuts, levels, bricks):
    ends = [max(1, round(c * (levels // bricks) / 8)) * bricks for c in cuts]
    return [(a, b) for a, b in zip([0] + ends[:-1], ends) if b > a]


def jobs_of(subs, levels, bricks):
    jobs = []
    for target in range(subs - 1, 0, -1):
        cuts = CUTS_LAST if target == subs - 1 else CUTS_FIRST
        jobs += [(f"s{target}l{a}", target - 1, target, a, b) for a, b in chunk_of(cuts, levels, bricks)]
    return jobs + [(f"s0l{a}", subs - 1, None, a, b) for a, b in chunk_of(CUTS_FIRST, levels, bricks)]


def on_device(increments, courant_x, courant_y, spectrum, vertical):
    subs, levels, rows, cols = increments.shape
    bricks, groups = lax.axis_size("brick"), lax.axis_size("sub")
    f32 = jnp.float32

    def neighbour(value, by, part_of_end):
        pairs = []
        for g in range(groups - 1 if part_of_end else groups):
            pairs += [(g * bricks + i, g * bricks + i + by) for i in range(bricks) if 0 <= i + by < bricks]
        return lax.ppermute(value, ("sub", "brick"), pairs)

    def next_sub(value):
        return lax.ppermute(value, "sub", [(i, i + 1) for i in range(groups - 1)])

    row_table, col_table = dct_table(rows * bricks), dct_table(cols)
    tables = (*halves(row_table), *halves(row_table.T), *halves(col_table), *halves(col_table.T))

    def cost(values, passes):
        return pl.CostEstimate(flops=20 * values * passes, bytes_accessed=16 * values * passes, transcendentals=0)

    parts = cols // LANES
    flat_all = [a.reshape(-1, cols) for a in (increments, courant_x, courant_y)]

    def pieces(array, sub, start):
        specs = [
            pl.BlockSpec((8 * STACK * rows, LANES), lambda i, j=j: ((sub * levels + start) // (8 * STACK) + i, j))
            for j in range(parts)
        ]
        return [array] * parts, specs

    def edges(sub, start, stop):
        size = 32
        block = lambda at: pl.BlockSpec((size, 8, cols), lambda i: ((sub * levels + start) // size + i, at, 0))
        arrays = [a.reshape(-1, rows, cols) for a in (increments, courant_x, courant_y)]
        return pl.pallas_call(
            edge_kernel,
            grid=((stop - start) // size,),
            in_specs=[block(rows // 8 - 1)] * 3 + [block(0)] * 3,
            out_specs=[pl.BlockSpec((3, size, cols), lambda i: (0, i, 0))] * 2,
            out_shape=[jax.ShapeDtypeStruct((3, stop - start, cols), f32)] * 2,
            compiler_params=params(),
            cost_estimate=pl.CostEstimate(flops=0, bytes_accessed=200 * (stop - start) * cols, transcendentals=0),
            name="edge",
        )(*arrays, *arrays)

    def tangent(number, sub, start, stop, state, halo, far, target):
        span = stop - start
        first = number == 0
        last = None if first else ("end" if target is None else "jump")
        slab = pl.BlockSpec((rows, 8 * STACK, cols), lambda i: (0, i, 0))
        inputs, specs = [], []

        def add(more, with_specs):
            inputs.extend(more)
            specs.extend(with_specs)

        if first:
            add(*pieces(flat_all[0], sub, start))
        else:
            add([state], [slab])
        add(*pieces(flat_all[1], sub, start))
        add(*pieces(flat_all[2], sub, start))
        add(halo, [pl.BlockSpec((halo[0].shape[0], 8 * STACK, cols), lambda i: (0, i, 0))] * 2)
        if not first:
            add(far, [pl.BlockSpec((1, 8 * STACK, cols), lambda i: (2, i, 0))] * 2)
        if last == "jump":
            add(*pieces(flat_all[0], target, start))
        if first:
            pair = pl.BlockSpec((2, 8 * STACK, cols), lambda i: (0, i, 0))
            out, out_spec = [(rows, span, cols)] + [(2, span, cols)] * 2, [slab, pair, pair]
        else:
            out, out_spec = [(span * rows, cols)], [pl.BlockSpec((8 * STACK * rows, cols), lambda i: (i, 0))]
        return pl.pallas_call(
            functools.partial(tangent_kernel, rows, parts, first, last),
            grid=(span // (8 * STACK),),
            in_specs=specs,
            out_specs=out_spec,
            out_shape=[jax.ShapeDtypeStruct(o, f32) for o in out],
            scratch_shapes=[
                pltpu.VMEM((rows + 2, 8, cols), f32),
                pltpu.VMEM((rows + 2, 8, cols), f32),
                pltpu.VMEM((rows, 8, cols), f32),
                pltpu.VMEM((rows, 8, cols), f32),
                pltpu.VMEM((parts, 8 * rows, LANES), f32),
            ],
            compiler_params=params(),
            cost_estimate=cost(span * rows * cols, 2),
            name="tangent",
        )(*inputs)

    def advance(sub, target, start, stop):
        low, high = edges(sub, start, stop)
        last = sub == subs - 1
        far = neighbour(low, 1, last), neighbour(high, -1, last)
        state, low, high = tangent(0, sub, start, stop, None, far, far, None)
        near = neighbour(low, 1, last), neighbour(high, -1, last)
        (moved,) = tangent(1, sub, start, stop, state, near, far, target)
        moved = moved.reshape(-1, rows, cols)
        if target is None:
            moved = increments[0, start:stop] - next_sub(moved)
        return moved

    def spread(value):
        return lax.all_to_all(value, "brick", split_axis=0, concat_axis=0, tiled=True)

    def middle(block, done, offset, total):
        share = block.shape[0] // bricks
        block = block.reshape(bricks, share, rows, cols)
        fixed = [pl.BlockSpec(t.shape, lambda i: (0, 0), pipeline_mode=pl.Buffered(1)) for t in (spectrum, *tables)]
        piece = pl.BlockSpec((bricks, 1, rows, cols), lambda i: (0, i, 0, 0))
        flops = 12 * share * bricks * rows * cols * (cols + bricks * rows)
        inputs = [block, spectrum, *tables]
        specs = [piece] + fixed
        kernel, alias = mid_kernel, {}
        if done is not None:
            alias = {len(inputs): 0}
            inputs.append(done)
            specs.append(pl.BlockSpec(memory_space=pl.ANY))
            kernel = lambda *refs: mid_kernel(*refs[:-2], refs[-1])
        return pl.pallas_call(
            kernel,
            grid=(share,),
            in_specs=specs,
            out_specs=pl.BlockSpec((bricks, 1, rows, cols), lambda i: (0, i + offset, 0, 0)),
            out_shape=jax.ShapeDtypeStruct((bricks, total, rows, cols), f32),
            input_output_aliases=alias,
            compiler_params=params(),
            cost_estimate=pl.CostEstimate(flops=flops, bytes_accessed=8 * block.size, transcendentals=0),
            name="middle",
        )(*inputs)

    def mix(field, sub, factor, old):
        field = field.reshape(levels, rows, cols)
        inputs = [field, *factor]
        whole = pl.BlockSpec((levels, levels), lambda i, j: (0, 0))
        specs = [pl.BlockSpec((levels, 8, LANES), lambda i, j: (0, j, i)), whole, whole]
        kernel, alias = mix_kernel, {}
        if old is not None:
            inputs.append(old)
            specs.append(pl.BlockSpec(memory_space=pl.ANY))
            alias = {3: 0}
        return pl.pallas_call(
            kernel,
            grid=(parts, rows // 8),
            in_specs=specs,
            out_specs=pl.BlockSpec((levels, 8, LANES), lambda i, j: (sub, j, i)),
            out_shape=jax.ShapeDtypeStruct((subs * levels, rows, cols), f32),
            input_output_aliases=alias,
            compiler_params=params(),
            cost_estimate=pl.CostEstimate(
                flops=6 * levels * levels * rows * cols, bytes_accessed=8 * levels * rows * cols, transcendentals=0
            ),
            name="mix",
        )(*inputs)

    out = None
    work = {}
    for name, sub, target, start, stop in jobs_of(subs, levels, bricks):
        moved = advance(sub, target, start, stop)
        block = spread(moved)
        work.setdefault(0 if target is None else target, []).append((name, start, stop, block))
    returned = []
    for sub, group in work.items():
        done, offset, columns = None, 0, []
        for name, a, b, block in group:
            share = (b - a) // bricks
            done = middle(block, done, offset, levels // bricks)
            offset += share
            columns.append(vertical[:, a:b].reshape(levels, bricks, share))
        factor = jnp.concatenate(columns, axis=2).reshape(levels, levels)
        returned.append((sub, halves(factor), spread(done)))
    for sub, factor, part in returned:
        out = mix(part, sub, factor, out)
    return out.reshape(increments.shape)


def solution(mesh):
    spec = P("sub", None, "brick", None)
    return jax.shard_map(
        on_device, mesh=mesh, in_specs=(spec, spec, spec, P(), P()), out_specs=spec, check_vma=False
    )
```
